128 devices in a mesh: ingest: 16 (over y, x), gr: 4 (over z), gc: 2 (over core).
Axes of the slice: x: 4, y: 4, z: 4, core: 2. Of those that a mesh axis runs over, the one named last changes fastest.
Arguments:
- embeddings: bfloat16 [131072, 768], P('ingest'), may hold values from -12 to 12
- cluster_ids: int32 [131072, 1], P('ingest'), may hold values from 0 to 127, as said below
- cluster_slots: int32 [128], replicated, may hold values from 0 to 127, each once
Outputs:
- mean_rows: bfloat16 [128, 2048, 768], P('ingest', 'gr', 'gc')
- dup_score: float32 [128, 2048], P('ingest', 'gr')
The draws below stay inside these ranges and needn't reach their ends.
Inputs may be any that keep to these rules, and one draw needn't show every extreme that they name: `cluster_ids`: within each shard of 8192 rows at most 128 rows fall in one cluster; one cluster has exactly 128 rows in every shard.
All inputs are finite; a program needn't handle non-finite values.
Results may differ from the reference program's by a relative error of at most 0.0034.
Values may be sent and summed in bfloat16 or wider, within the bound.
No kernel may reach another device: no remote copies, remote signals or barrier semaphores. Data moves between devices by JAX's collectives and lax.ppermute only.
A program may use at most 128 MiB of HBM per device.

```python
import math
import jax
import jax.numpy as jnp
from jax import lax

D = 768
PER_SRC = 128
CLUSTERS = 128
CAP = 2048
ROWS_DEV = 8192
ROWS = 131072
N_INGEST = 16


def common_clusters(key):
    order_key, share_key, shuffle_key = jax.random.split(key, 3)
    shard_count = ROWS // ROWS_DEV
    half_count = CLUSTERS // 2
    ranking = jax.random.permutation(order_key, CLUSTERS)
    ladder = jnp.arange(half_count, dtype=jnp.int32)
    reach_top = 1 + (PER_SRC - 1) * ladder // max(half_count - 1, 1)
    taken = jax.random.randint(share_key, (shard_count, half_count), 0, reach_top[None, :], dtype=jnp.int32)
    by_rank = jnp.concatenate([PER_SRC - taken, taken[:, ::-1]], axis=1).astype(jnp.int32)
    counts = jnp.zeros((shard_count, CLUSTERS), jnp.int32).at[:, ranking].set(by_rank)
    boundary = jnp.cumsum(counts, axis=1)
    position = jnp.arange(ROWS_DEV, dtype=jnp.int32)
    ordered = jnp.sum((boundary[:, None, :] <= position[None, :, None]).astype(jnp.int32), axis=2)
    shuffled = jax.random.permutation(shuffle_key, ordered, axis=1, independent=True)
    return shuffled.reshape(ROWS, 1).astype(jnp.int32)


def draw_cluster_ids(key, part):
    return common_clusters(jax.random.fold_in(key, 11))


def draw_embeddings(key, part):
    cluster_of = common_clusters(jax.random.fold_in(key, 11))[:, 0]
    keys = jax.random.split(jax.random.fold_in(key, 23), 5)
    group_count = max(CAP // 4, 8)
    centroids = jax.random.normal(keys[0], (CLUSTERS, D), jnp.float32)
    group_vectors = jax.random.normal(keys[1], (group_count, D), jnp.float32)
    group_of = jax.random.randint(keys[2], (ROWS,), 0, group_count, dtype=jnp.int32)
    spread = jnp.exp(jax.random.uniform(keys[3], (ROWS, 1), jnp.float32, math.log(0.1), math.log(0.6)))
    noise = jax.random.normal(keys[4], (ROWS, D), jnp.float32)
    scaling = jnp.ones((ROWS, 1), jnp.float32)
    values = 0.6 * centroids[cluster_of] + 0.75 * group_vectors[group_of] + spread * noise
    lengths = jnp.sqrt(jnp.sum(values * values, axis=1, keepdims=True))
    values = values * (math.sqrt(D) / lengths) * scaling
    return jnp.clip(values, -12.0, 12.0).astype(jnp.bfloat16)


def setup_inputs(seed: int = 0) -> dict:
    seeds = jax.random.split(jax.random.key(seed), 4)
    embeddings = draw_embeddings(jax.random.fold_in(seeds[3], 71), 0)
    cluster_ids = draw_cluster_ids(jax.random.fold_in(seeds[3], 71), 0)
    cluster_slots = jax.random.permutation(seeds[2], CLUSTERS).astype(jnp.int32)
    return dict(embeddings=embeddings, cluster_ids=cluster_ids, cluster_slots=cluster_slots)


sharpness = 8.0
epsilon = 1e-06

def per_cluster(pair):
    cluster_rows, occupied = pair
    widened = cluster_rows.astype(jnp.float32)
    squares = lax.optimization_barrier(jnp.sum(widened * widened, axis=1, keepdims=True))
    normed = (widened * lax.rsqrt(squares + epsilon)).astype(jnp.bfloat16)
    cosine = jnp.dot(normed, normed.T, preferred_element_type=jnp.float32)
    weights = occupied[:, None] * occupied[None, :] * jnp.exp(sharpness * (cosine - 1.0))
    row_total = lax.optimization_barrier(jnp.sum(weights, axis=1))
    neighbour = jnp.dot(weights.astype(jnp.bfloat16), cluster_rows, preferred_element_type=jnp.float32)
    divisor = row_total + 1.0 - occupied
    return ((neighbour / divisor[:, None]).astype(jnp.bfloat16), jnp.log(divisor))

def reference(embeddings, cluster_ids, cluster_slots):
    sources = N_INGEST
    capacity = sources * PER_SRC
    cluster_of = cluster_ids.reshape(sources, ROWS_DEV)
    onehot = (cluster_of[:, :, None] == jnp.arange(CLUSTERS, dtype=jnp.int32)[None, None, :]).astype(jnp.int32)
    row_rank = lax.optimization_barrier(jnp.sum(jnp.cumsum(onehot, axis=1) * onehot, axis=2)) - 1
    counts = lax.optimization_barrier(jnp.sum(onehot, axis=1))
    slot_of = cluster_slots[cluster_of]
    position = (slot_of * sources + jnp.arange(sources, dtype=jnp.int32)[:, None]) * PER_SRC + row_rank
    blocks = jnp.zeros((CLUSTERS * capacity, D), jnp.bfloat16).at[position.reshape(-1).astype(jnp.int32)].set(embeddings)
    blocks = blocks.reshape(CLUSTERS, capacity, D)
    slot_counts = jnp.zeros((CLUSTERS, sources), jnp.int32).at[cluster_slots].set(counts.T)
    occupied = jnp.arange(PER_SRC, dtype=jnp.int32)[None, None, :] < slot_counts[:, :, None]
    occupied = occupied.reshape(CLUSTERS, capacity).astype(jnp.float32)
    mean_rows, dup_score = lax.map(per_cluster, (blocks, occupied))
    return (mean_rows, dup_score)
```

```python
import functools
import jax
import jax.numpy as jnp
from jax import lax
from jax.experimental import pallas as pl
from jax.experimental.pallas import tpu as pltpu
from jax.sharding import PartitionSpec as P

D = 768
NT=(((1,),(1,)),((),()))
NN=(((1,),(0,)),((),()))
bf16=jnp.bfloat16; f32=jnp.float32
ROWS=8192; CH=ROWS//128; NSEG=8; W=64; CPAD=2048+W
def dot(a,b,dn=NN): return lax.dot_general(a,b,dn,preferred_element_type=f32)
def iota(shape,d): return lax.broadcasted_iota(jnp.int32,shape,d)
def gk(par, ids_ref, slots_ref, emb_ref, out_ref, C, emb_v, ev, rt, gref, base_v, base_s, inv_s, sem, dsem, *, NK, PR):
    NG=16*NK
    seg=ROWS//NSEG
    cps=[pltpu.make_async_copy(emb_ref.at[pl.ds(s*seg,seg)],emb_v.at[pl.ds(s*seg,seg)],sem.at[s]) for s in range(NSEG)]
    for c in cps: c.start()
    C[...]=jnp.zeros_like(C)
    gi=iota((NG,128),0)
    want=(gi%16)*8+par[0]+gi//16
    cl=jnp.sum(jnp.where(slots_ref[...]==want,iota((NG,128),1),0),axis=1,keepdims=True)
    ids=ids_ref[...]
    E=(ids[:,None,:]==cl[None,:,:]).astype(f32)
    Eb=E.astype(bf16).reshape(CH*NG,128)
    U=(iota((128,128),0)<iota((128,128),1)).astype(bf16)
    ONE=jnp.ones((128,128),bf16)
    pre=dot(Eb,U).reshape(CH,NG,128)
    tot=dot(Eb,ONE).reshape(CH,NG,128)
    roff=par[1].astype(f32)
    carry=jnp.zeros((NG,128),f32)-roff
    ranks=[];vals=[];hotv=[]
    for a in range(CH):
        r=carry+pre[a]
        carry=carry+tot[a]
        e=E[a]
        v=jnp.where((r>=0)&(r<PR),e,0.0)
        hotv.append(v)
        ranks.append(jnp.sum(v*(r+1.0),axis=0,keepdims=True)-1.0)
        vals.append(jnp.sum(v,axis=0,keepdims=True))
    rank_row=jnp.concatenate(ranks,axis=0)
    vrow=jnp.concatenate(vals,axis=0)
    vb=vrow.astype(bf16)
    pg=dot(vb,U)
    tb=dot(vb,ONE).astype(bf16)
    L=(iota((CH,CH),1)<iota((CH,CH),0)).astype(bf16)
    g=dot(L,tb)+pg
    gref[...]=jnp.where(vrow>0,g,-1e6).astype(jnp.int32)
    trow=dot(jnp.ones((8,128),bf16),vb,NT).astype(bf16)
    UC=(iota((CH,128),0)<iota((CH,128),1)).astype(bf16)
    base_v[...]=dot(trow,UC).astype(jnp.int32)
    cp=pltpu.make_async_copy(base_v,base_s,dsem)
    cp.start()
    val=g+1.0
    hi=jnp.floor(val*(1.0/64.0)); lo=val-64.0*hi
    pi=iota((PR,128),0).astype(f32)
    for a in range(CH):
        rt[:,a*128:(a+1)*128]=(rank_row[a:a+1]==pi).astype(bf16)
        ev[0:NG,a*128:(a+1)*128]=(hotv[a]*hi[a:a+1]).astype(bf16)
        ev[NG:2*NG,a*128:(a+1)*128]=(hotv[a]*lo[a:a+1]).astype(bf16)
    hl=dot(rt[...],ev[...],NT)
    inv_s[...]=64.0*hl[:,:NG]+hl[:,NG:]-1.0
    cp.wait()
    ji=iota((W,256),0)
    cps_per=seg//256
    for s in range(NSEG):
        cps[s].wait()
        def body(i,_):
            b0=base_s[0,2*i]; b1=base_s[0,2*i+2]
            al=(b0//16)*16
            nw=jnp.where(b1>b0,(b1-al+W-1)//W,0)
            gr=jnp.concatenate([gref[pl.ds(2*i,1),:],gref[pl.ds(2*i+1,1),:]],axis=1)
            x=emb_v[pl.ds(pl.multiple_of(i*256,256),256),:]
            def win(w,_):
                st=pl.multiple_of(al+w*W,16)
                p=((gr-st)==ji).astype(f32).astype(bf16)
                y=dot(p,x).astype(bf16)
                C[pl.ds(st,W),:]=C[pl.ds(st,W),:]+y
                return 0
            lax.fori_loop(0,nw,win,0)
            return 0
        lax.fori_loop(s*cps_per,(s+1)*cps_per,body,0)
    nm=base_s[0,CH]
    GB=256//PR
    def perm(K):
        def tile(n,_):
            cols=[]
            for u in range(GB):
                cols.append(jnp.sum(jnp.where(iota((PR,NG),1)==n*GB+u,inv_s[...],0.0),axis=1,keepdims=True))
            col=jnp.concatenate(cols,axis=0)
            ki=iota((256,K),1).astype(f32)
            p=(col==ki).astype(bf16)
            y=dot(p,C[0:K,:])
            o=pl.multiple_of(n*256,256)
            out_ref[pl.ds(o,256),:]=y.astype(bf16)
            h=y[:,0:128]+jnp.where((col<0.0)&(iota((256,128),1)==0),64.0,0.0)
            out_ref[pl.ds(o,256),0:128]=h.astype(bf16)
            return 0
        lax.fori_loop(0,NG//GB,tile,0)
    @pl.when(nm<=1280)
    def _(): perm(1280)
    @pl.when(nm>1280)
    def _(): perm(2048)
def gather(par,ids,slots,emb,NK,PR):
    NG=16*NK
    return pl.pallas_call(functools.partial(gk,NK=NK,PR=PR),
      in_specs=[pl.BlockSpec(memory_space=pltpu.SMEM),pl.BlockSpec(memory_space=pltpu.VMEM),pl.BlockSpec(memory_space=pltpu.VMEM),pl.BlockSpec(memory_space=pl.ANY)],
      out_specs=pl.BlockSpec(memory_space=pltpu.VMEM),
      out_shape=jax.ShapeDtypeStruct((NG*PR,D),bf16),
      scratch_shapes=[pltpu.VMEM((CPAD,D),bf16),pltpu.VMEM((ROWS,D),bf16),pltpu.VMEM((2*NG,ROWS),bf16),pltpu.VMEM((PR,ROWS),bf16),
        pltpu.VMEM((CH,128),jnp.int32),pltpu.VMEM((8,128),jnp.int32),pltpu.SMEM((8,128),jnp.int32),pltpu.VMEM((PR,NG),f32),
        pltpu.SemaphoreType.DMA((NSEG,)),pltpu.SemaphoreType.DMA],
      compiler_params=pltpu.CompilerParams(vmem_limit_bytes=60<<20),
      )(par,ids.reshape(CH,128),slots.reshape(1,128),emb)
CAP = 2048
LOG2E = 1.4426950408889634


def ck(x_ref, out_ref, sc_ref, normed, bias, *, bq):
    i = pl.program_id(0)

    @pl.when(i == 0)
    def _():
        for k in range(CAP // 256):
            s = pl.ds(k * 256, 256)
            v = x_ref[s, :].astype(f32)
            sq = jnp.sum(v * v, axis=1, keepdims=True)
            normed[s, :] = (v * lax.rsqrt(sq + 1e-6)).astype(bf16)
        e0 = (iota((8, D), 1) == 0).astype(bf16)
        f0 = dot(e0, x_ref[...], NT)
        bias[...] = jnp.where(f0 > 32.0, -1e30, -8.0 * LOG2E)

    q = normed[pl.ds(i * bq, bq), :]
    cos = dot(q, normed[...], NT)
    w = jnp.exp2(cos * (8.0 * LOG2E) + bias[0:1, :])
    tot = jnp.sum(w, axis=1, keepdims=True)
    nb = dot(w.astype(bf16), x_ref[...])
    un = x_ref[pl.ds(i * bq, bq), 0:1].astype(f32) > 32.0
    div = jnp.where(un, 1.0, tot)
    m = jnp.where(un, 0.0, nb / div).astype(bf16)
    out_ref[0, 0] = m[:, :384]
    out_ref[0, 1] = m[:, 384:]
    sc_ref[...] = jnp.broadcast_to(jnp.log(div), (bq, 128)).T[0:1, :].reshape(1, 1, bq)


def cluster(x, bq=512):
    n = CAP // bq
    per = 512 // bq
    return pl.pallas_call(
        functools.partial(ck, bq=bq),
        grid=(n,),
        in_specs=[pl.BlockSpec((CAP, D), lambda i: (0, 0))],
        out_specs=[
            pl.BlockSpec((1, 2, bq, 384), lambda i: (i // per, 0, i % per, 0)),
            pl.BlockSpec((1, 1, bq), lambda i: (i, 0, 0)),
        ],
        out_shape=[
            jax.ShapeDtypeStruct((4, 2, 512, 384), bf16),
            jax.ShapeDtypeStruct((n, 1, bq), f32),
        ],
        scratch_shapes=[pltpu.VMEM((CAP, D), bf16), pltpu.VMEM((8, CAP), f32)],
        compiler_params=pltpu.CompilerParams(vmem_limit_bytes=60 << 20),
        cost_estimate=pl.CostEstimate(
            flops=4 * CAP * CAP * D, bytes_accessed=4 * CAP * D, transcendentals=CAP * CAP
        ),
    )(x)


def on_device(embeddings, cluster_ids, cluster_slots):
    member = lax.axis_index("gr") * 2 + lax.axis_index("gc")
    par = jnp.stack([member, member * 0]).astype(jnp.int32)
    outgoing = gather(par, cluster_ids, cluster_slots, embeddings, 1, 128)
    arrived = lax.all_to_all(
        outgoing.reshape(16, 128, D), "ingest", split_axis=0, concat_axis=0, tiled=True
    )
    means, scores = cluster(arrived.reshape(CAP, D))
    tiles = means.reshape(8, 1, 512, 384)
    score_tiles = jnp.broadcast_to(scores.reshape(4, 1, 1, 512), (4, 2, 1, 512)).reshape(8, 1, 512)
    mean_rows = lax.all_to_all(tiles, ("gr", "gc"), split_axis=0, concat_axis=0, tiled=True)
    dup_score = lax.all_to_all(score_tiles, ("gr", "gc"), split_axis=0, concat_axis=0, tiled=True)
    return (mean_rows.reshape(8, 512, 384), dup_score.reshape(8, 512))


def solution(mesh):
    return jax.shard_map(
        on_device,
        mesh=mesh,
        in_specs=(P("ingest", None), P("ingest", None), P()),
        out_specs=(P("ingest", "gr", "gc"), P("ingest", "gr")),
        check_vma=False,
    )
```

```python
import jax
import jax.numpy as jnp
from jax import lax
from jax.experimental import pallas as pl
from jax.experimental.pallas import tpu as pltpu
from jax.sharding import PartitionSpec as P

D = 768
NT = (((1,), (1,)), ((), ()))
NN = (((1,), (0,)), ((), ()))
bf16 = jnp.bfloat16
f32 = jnp.float32


def dot(a, b, dn=NN):
    return lax.dot_general(a, b, dn, preferred_element_type=f32)


def iota(shape, d):
    return lax.broadcasted_iota(jnp.int32, shape, d)


ROWS = 8192
CH = ROWS // 128
NSEG = 8
NL = 4
GL = 16 // NL
W = 48
PR = 128
LCAP = GL * PR
CPAD = LCAP + 64


def gk(par, ids_ref, slots_ref, emb_ref, out_ref, C, emb_v, ev, rt, gref, rk, base_v, base_s, stage, sem, dsem, osem):
    seg = ROWS // NSEG
    cps = [
        pltpu.make_async_copy(
            emb_ref.at[pl.ds(s * seg, seg)], emb_v.at[pl.ds(s * seg, seg)], sem.at[s]
        )
        for s in range(NSEG)
    ]
    for c in cps:
        c.start()
    C[...] = jnp.zeros_like(C)
    want = iota((16, 128), 0) * 8 + par[0]
    cl = jnp.sum(jnp.where(slots_ref[...] == want, iota((16, 128), 1), 0), axis=1, keepdims=True)
    hot = (ids_ref[...][:, None, :] == cl[None, :, :]).astype(f32)
    hotb = hot.astype(bf16).reshape(CH * 16, 128)
    upper = (iota((128, 128), 0) < iota((128, 128), 1)).astype(bf16)
    ones = jnp.ones((128, 128), bf16)
    pre = dot(hotb, upper).reshape(CH, 16, 128)
    tot = dot(hotb, ones).reshape(CH, 16, 128)
    carry = jnp.ones((16, 128), f32)
    for a in range(CH):
        rk[a] = carry + pre[a]
        carry = carry + tot[a]
    own = (hot * rk[...]).astype(bf16).reshape(CH * 16, 128)
    r4 = iota((NL * CH, CH * 16), 0)
    c4 = iota((NL * CH, CH * 16), 1)
    pick = (((c4 >> 4) == (r4 & 63)) & (((c4 & 15) >> 2) == (r4 >> 6))).astype(bf16)
    rank4 = dot(pick, own)
    valid = rank4 > 0.0
    vb = valid.astype(f32).astype(bf16)
    rr = iota((NL * CH, NL * CH), 0)
    cc = iota((NL * CH, NL * CH), 1)
    lower = (((rr >> 6) == (cc >> 6)) & (cc < rr)).astype(bf16)
    tb = dot(vb, ones).astype(bf16)
    g = dot(lower, tb) + dot(vb, upper)
    gref[...] = jnp.where(valid, g, -1e6).astype(jnp.int32)
    trow = dot(jnp.ones((8, 128), bf16), vb, NT).astype(bf16)
    before = (iota((CH, 128), 0) < iota((CH, 128), 1)).astype(bf16)
    after = (iota((CH, 128), 0) < iota((CH, 128), 1) + 2).astype(bf16)
    lane = iota((8, 128), 1)
    chunk = (lane < CH) & ((lane & 1) == 0)
    over = jnp.zeros((8, 128), jnp.int32)
    for l in range(NL):
        counts = trow[:, l * CH : (l + 1) * CH]
        base = dot(counts, before).astype(jnp.int32)
        need = dot(counts, after).astype(jnp.int32) - (base & -16)
        over = jnp.maximum(over, jnp.where(chunk, need, 0))
        base_v[l * 8 : l * 8 + 8] = base
    cp = pltpu.make_async_copy(base_v, base_s, dsem)
    cp.start()
    rank = rank4[0:CH]
    val = jnp.where(valid[0:CH], g[0:CH] + 1.0, 0.0)
    for l in range(1, NL):
        s = slice(l * CH, (l + 1) * CH)
        rank = rank + rank4[s]
        val = val + jnp.where(valid[s], g[s] + 1.0, 0.0)
    hi = jnp.floor(val * (1.0 / 64.0))
    lo = val - 64.0 * hi
    pi = (iota((PR, 128), 0) + 1).astype(f32)
    for a in range(CH):
        s = slice(a * 128, (a + 1) * 128)
        rt[:, s] = (rank[a : a + 1] == pi).astype(bf16)
        ev[0:16, s] = (hot[a] * hi[a : a + 1]).astype(bf16)
        ev[16:32, s] = (hot[a] * lo[a : a + 1]).astype(bf16)
    hl = dot(rt[...], ev[...], NT)
    inv = 64.0 * hl[:, :16] + hl[:, 16:] - 1.0
    cp.wait()
    ji = iota((W, 256), 0)

    def window(i, l, w):
        al = base_s[l * 8, 2 * i] & -16
        return pl.multiple_of(al + w * W, 16)

    def grow(i, l):
        k = l * CH + 2 * i
        return jnp.concatenate([gref[pl.ds(k, 1), :], gref[pl.ds(k + 1, 1), :]], axis=1)

    UN = 4
    steps = seg // 256 // UN
    for s in range(NSEG):
        cps[s].wait()

        def body(j, _):
            for u in range(UN):
                i = j * UN + u
                x = emb_v[pl.ds(pl.multiple_of(i * 256, 256), 256), :]
                st = [window(i, l, 0) for l in range(NL)]
                p = jnp.concatenate(
                    [(grow(i, l) - st[l] == ji).astype(f32).astype(bf16) for l in range(NL)], axis=0
                )
                y = dot(p, x).astype(bf16)
                for l in range(NL):
                    C[l, pl.ds(st[l], W), :] = C[l, pl.ds(st[l], W), :] + y[l * W : (l + 1) * W]
            return 0

        lax.fori_loop(s * steps, (s + 1) * steps, body, 0)

    def rest(i, _):
        for l in range(NL):
            b0 = base_s[l * 8, 2 * i]
            need = base_s[l * 8, 2 * i + 2] - (b0 & -16)

            @pl.when(need > W)
            def _():
                x = emb_v[pl.ds(pl.multiple_of(i * 256, 256), 256), :]

                def win(w, _):
                    st = window(i, l, w)
                    y = dot((grow(i, l) - st == ji).astype(f32).astype(bf16), x).astype(bf16)
                    C[l, pl.ds(st, W), :] = C[l, pl.ds(st, W), :] + y
                    return 0

                lax.fori_loop(1, (need + W - 1) // W, win, 0)

        return 0

    @pl.when(jnp.max(over) > W)
    def _():
        lax.fori_loop(0, CH // 2, rest, 0)

    ki = iota((LCAP, LCAP), 1).astype(f32)
    first = iota((LCAP, 128), 1) == 0
    outs = []
    for l in range(NL):
        col = jnp.concatenate([inv[:, t : t + 1] for t in range(l * GL, (l + 1) * GL)], axis=0)
        y = dot((col == ki).astype(f32).astype(bf16), C[l, 0:LCAP, :])
        mark = y[:, 0:128] + jnp.where((col < 0.0) & first, 64.0, 0.0)
        stage[l, :, 0:128] = mark.astype(bf16)
        stage[l, :, 128:D] = y[:, 128:D].astype(bf16)
        cp = pltpu.make_async_copy(stage.at[l], out_ref.at[pl.ds(l * LCAP, LCAP)], osem.at[l])
        cp.start()
        outs.append(cp)
    for cp in outs:
        cp.wait()


def gather(par, ids, slots, emb):
    return pl.pallas_call(
        gk,
        in_specs=[
            pl.BlockSpec(memory_space=pltpu.SMEM),
            pl.BlockSpec(memory_space=pltpu.VMEM),
            pl.BlockSpec(memory_space=pltpu.VMEM),
            pl.BlockSpec(memory_space=pl.ANY),
        ],
        out_specs=pl.BlockSpec(memory_space=pltpu.HBM),
        out_shape=jax.ShapeDtypeStruct((16 * PR, D), bf16),
        scratch_shapes=[
            pltpu.VMEM((NL, CPAD, D), bf16),
            pltpu.VMEM((ROWS, D), bf16),
            pltpu.VMEM((32, ROWS), bf16),
            pltpu.VMEM((PR, ROWS), bf16),
            pltpu.VMEM((NL * CH, 128), jnp.int32),
            pltpu.VMEM((CH, 16, 128), f32),
            pltpu.VMEM((NL * 8, 128), jnp.int32),
            pltpu.SMEM((NL * 8, 128), jnp.int32),
            pltpu.VMEM((NL, LCAP, D), bf16),
            pltpu.SemaphoreType.DMA((NSEG,)),
            pltpu.SemaphoreType.DMA,
            pltpu.SemaphoreType.DMA((NL,)),
        ],
        compiler_params=pltpu.CompilerParams(vmem_limit_bytes=60 << 20),
    )(par, ids.reshape(CH, 128), slots.reshape(1, 128), emb)


CAP = 2048
BQ = 512
LOG2E = 1.4426950408889634
VM = pl.BlockSpec(memory_space=pltpu.VMEM)
SM = pl.BlockSpec(memory_space=pltpu.SMEM)
HB = pl.BlockSpec(memory_space=pltpu.HBM)
TILE = jax.ShapeDtypeStruct((BQ, 384), bf16)
SCORE = jax.ShapeDtypeStruct((1, BQ), f32)


def rows_of(k):
    return pl.ds(pl.multiple_of(k % 4 * BQ, BQ), BQ)


def finish(r, c, x_ref, tot, nb, keep_ref, swap_ref, sc_ref):
    un = x_ref[rows_of(r), 0:128][:, 0:1].astype(f32) > 32.0
    div = jnp.where(un, 1.0, tot)
    m = jnp.where(un, 0.0, nb / div).astype(bf16)
    lo, hi = m[:, :384], m[:, 384:]
    keep_ref[...] = jnp.where(c == 0, lo, hi)
    swap_ref[...] = jnp.where(c == 0, hi, lo)
    sc_ref[...] = jnp.broadcast_to(jnp.log(div), (BQ, 128)).T[0:1, :]


def query_block(r, c, x_ref, normed, bias, keep_ref, swap_ref, sc_ref):
    cos = dot(normed[rows_of(r), :], normed[...], NT)
    w = jnp.exp2(cos * (8.0 * LOG2E) + bias[0:1, :])
    tot = jnp.sum(w, axis=1, keepdims=True)
    nb = dot(w.astype(bf16), x_ref[...])
    finish(r, c, x_ref, tot, nb, keep_ref, swap_ref, sc_ref)


def query_block_fresh(r, c, x_ref, normed, bias, keep_ref, swap_ref, sc_ref):
    tot = jnp.zeros((BQ, 1), f32)
    nb = jnp.zeros((BQ, D), f32)
    e0 = (iota((8, D), 1) == 0).astype(bf16)
    for k in range(4):
        s = rows_of(r + k)
        x = x_ref[s, :]
        v = x.astype(f32)
        n = (v * lax.rsqrt(jnp.sum(v * v, axis=1, keepdims=True) + 1e-6)).astype(bf16)
        normed[s, :] = n
        b = jnp.where(dot(e0, x, NT) > 32.0, -1e30, -8.0 * LOG2E)
        bias[:, s] = b
        if k == 0:
            q = n
        w = jnp.exp2(dot(q, n, NT) * (8.0 * LOG2E) + b[0:1, :])
        tot = tot + jnp.sum(w, axis=1, keepdims=True)
        nb = nb + dot(w.astype(bf16), x)
    finish(r, c, x_ref, tot, nb, keep_ref, swap_ref, sc_ref)


def cost(blocks):
    return pl.CostEstimate(
        flops=4 * blocks * BQ * CAP * D,
        bytes_accessed=4 * CAP * D,
        transcendentals=blocks * BQ * CAP,
    )


def params():
    return pltpu.CompilerParams(vmem_limit_bytes=28 << 20)


def first_block(par, x):
    def kernel(p, x_ref, normed, bias, keep, swap, sc):
        query_block_fresh(p[1] + 2, p[2], x_ref, normed, bias, keep, swap, sc)

    return pl.pallas_call(
        kernel,
        in_specs=[SM, VM],
        out_specs=[VM] * 5,
        out_shape=[
            jax.ShapeDtypeStruct((CAP, D), bf16),
            jax.ShapeDtypeStruct((8, CAP), f32),
            TILE,
            TILE,
            SCORE,
        ],
        compiler_params=params(),
        cost_estimate=cost(1),
    )(par, x)


def next_blocks(par, x, normed, bias):
    def kernel(p, x_ref, normed, bias, k1, s1, c1, k3, s3, c3):
        query_block(p[1] + 1, p[2], x_ref, normed, bias, k1, s1, c1)
        query_block(p[1] + 3, p[2], x_ref, normed, bias, k3, s3, c3)

    return pl.pallas_call(
        kernel,
        in_specs=[SM, VM, VM, VM],
        out_specs=[VM] * 6,
        out_shape=[TILE, TILE, SCORE] * 2,
        compiler_params=params(),
        cost_estimate=cost(2),
    )(par, x, normed, bias)


def own_block(par, x, normed, bias, others):
    def kernel(p, x_ref, normed, bias, c1, c2, c3, out_ref, s0, scores, tile, c0, sem):
        query_block(p[1], p[2], x_ref, normed, bias, tile, s0, c0)
        cp = pltpu.make_async_copy(tile, out_ref.at[p[0]], sem)
        cp.start()
        for d, sc in enumerate((c0, c1, c2, c3)):
            for h in range(2):
                scores[(p[1] + d) % 4 * 2 + h] = sc[...]
        cp.wait()

    return pl.pallas_call(
        kernel,
        in_specs=[SM] + [VM] * 6,
        out_specs=[HB, VM, VM],
        out_shape=[
            jax.ShapeDtypeStruct((8, BQ, 384), bf16),
            TILE,
            jax.ShapeDtypeStruct((8, 1, BQ), f32),
        ],
        scratch_shapes=[
            pltpu.VMEM((BQ, 384), bf16),
            pltpu.VMEM((1, BQ), f32),
            pltpu.SemaphoreType.DMA,
        ],
        compiler_params=params(),
        cost_estimate=cost(1),
    )(par, x, normed, bias, *others)


def place(par, out, got):
    n = len(got)

    def kernel(p, *refs):
        out_ref, sem = refs[n + 1], refs[n + 2]
        cps = []
        for i, (dz, dc, _) in enumerate(got):
            at = (p[1] + 4 - dz) % 4 * 2 + (p[2] + dc) % 2
            cps.append(pltpu.make_async_copy(refs[i], out_ref.at[at], sem.at[i]))
            cps[-1].start()
        for cp in cps:
            cp.wait()

    return pl.pallas_call(
        kernel,
        in_specs=[SM] + [VM] * n + [HB],
        out_specs=HB,
        out_shape=jax.ShapeDtypeStruct(out.shape, out.dtype),
        input_output_aliases={n + 1: 0},
        scratch_shapes=[pltpu.SemaphoreType.DMA((n,))],
        compiler_params=pltpu.CompilerParams(vmem_limit_bytes=8 << 20),
    )(par, *[p for _, _, p in got], out)


def step(embeddings, cluster_ids, cluster_slots):
    z, c = lax.axis_index("gr"), lax.axis_index("gc")
    par = jnp.stack([z * 2 + c, z, c]).astype(jnp.int32)
    outgoing = gather(par, cluster_ids, cluster_slots, embeddings)
    arrived = lax.all_to_all(
        outgoing.reshape(16, PR, D), "ingest", split_axis=0, concat_axis=0, tiled=True
    )
    arrived, par = lax.optimization_barrier((arrived, par))
    x = arrived.reshape(CAP, D)

    def send(a, dz, dc):
        pairs = [(i, (i // 2 + dz) % 4 * 2 + (i % 2 + dc) % 2) for i in range(8)]
        return (dz, dc, lax.ppermute(a, ("gr", "gc"), pairs))

    normed, bias, k2, s2, c2 = first_block(par, x)
    got = [send(k2, 2, 0), send(s2, 2, 1)]
    k1, s1, c1, k3, s3, c3 = next_blocks(par, x, normed, bias)
    got += [send(k1, 1, 0), send(k3, 3, 0), send(s1, 1, 1), send(s3, 3, 1)]
    out, s0, scores = own_block(par, x, normed, bias, (c1, c2, c3))
    got += [send(s0, 0, 1)]
    dup_score = lax.all_to_all(scores, ("gr", "gc"), split_axis=0, concat_axis=0, tiled=True)
    out = place(par, out, got[:2])
    out = place(par, out, got[2:])
    return (out, dup_score.reshape(8, BQ))


def solution(mesh):
    return jax.shard_map(
        step,
        mesh=mesh,
        in_specs=(P("ingest", None), P("ingest", None), P()),
        out_specs=(P("ingest", "gr", "gc"), P("ingest", "gr")),
        check_vma=False,
    )
```

```python
import jax
import jax.numpy as jnp
from jax import lax
from jax.experimental import pallas as pl
from jax.experimental.pallas import tpu as pltpu
from jax.sharding import PartitionSpec as P

D = 768
NT = (((1,), (1,)), ((), ()))
NN = (((1,), (0,)), ((), ()))
bf16 = jnp.bfloat16
f32 = jnp.float32


def dot(a, b, dn=NN):
    return lax.dot_general(a, b, dn, preferred_element_type=f32)


def iota(shape, d):
    return lax.broadcasted_iota(jnp.int32, shape, d)


ROWS = 8192
CH = ROWS // 128
NSEG = 8
NL = 4
GL = 16 // NL
W = 48
PR = 128
LCAP = GL * PR
CPAD = LCAP + 64


def gk(ids_ref, slots_ref, emb_ref, out_ref, C, emb_v, ev, rt, gref, rk, base_v, base_s, stage, sem, dsem, osem):
    seg = ROWS // NSEG
    cps = [
        pltpu.make_async_copy(
            emb_ref.at[pl.ds(s * seg, seg)], emb_v.at[pl.ds(s * seg, seg)], sem.at[s]
        )
        for s in range(NSEG)
    ]
    for c in cps:
        c.start()
    C[...] = jnp.zeros_like(C)
    want = iota((16, 128), 0) * 8 + lax.axis_index("gr") * 2 + lax.axis_index("gc")
    cl = jnp.sum(jnp.where(slots_ref[...] == want, iota((16, 128), 1), 0), axis=1, keepdims=True)
    hot = (ids_ref[...][:, None, :] == cl[None, :, :]).astype(f32)
    hotb = hot.astype(bf16).reshape(CH * 16, 128)
    upper = (iota((128, 128), 0) < iota((128, 128), 1)).astype(bf16)
    ones = jnp.ones((128, 128), bf16)
    pre = dot(hotb, upper).reshape(CH, 16, 128)
    tot = dot(hotb, ones).reshape(CH, 16, 128)
    carry = jnp.ones((16, 128), f32)
    for a in range(CH):
        rk[a] = carry + pre[a]
        carry = carry + tot[a]
    own = (hot * rk[...]).astype(bf16).reshape(CH * 16, 128)
    r4 = iota((NL * CH, CH * 16), 0)
    c4 = iota((NL * CH, CH * 16), 1)
    pick = (((c4 >> 4) == (r4 & 63)) & (((c4 & 15) >> 2) == (r4 >> 6))).astype(bf16)
    rank4 = dot(pick, own)
    valid = rank4 > 0.0
    vb = valid.astype(f32).astype(bf16)
    rr = iota((NL * CH, NL * CH), 0)
    cc = iota((NL * CH, NL * CH), 1)
    lower = (((rr >> 6) == (cc >> 6)) & (cc < rr)).astype(bf16)
    tb = dot(vb, ones).astype(bf16)
    g = dot(lower, tb) + dot(vb, upper)
    gref[...] = jnp.where(valid, g, -1e6).astype(jnp.int32)
    trow = dot(jnp.ones((8, 128), bf16), vb, NT).astype(bf16)
    before = (iota((CH, 128), 0) < iota((CH, 128), 1)).astype(bf16)
    after = (iota((CH, 128), 0) < iota((CH, 128), 1) + 2).astype(bf16)
    lane = iota((8, 128), 1)
    chunk = (lane < CH) & ((lane & 1) == 0)
    over = jnp.zeros((8, 128), jnp.int32)
    for l in range(NL):
        counts = trow[:, l * CH : (l + 1) * CH]
        base = dot(counts, before).astype(jnp.int32)
        need = dot(counts, after).astype(jnp.int32) - (base & -16)
        over = jnp.maximum(over, jnp.where(chunk, need, 0))
        base_v[l * 8 : l * 8 + 8] = base
    cp = pltpu.make_async_copy(base_v, base_s, dsem)
    cp.start()
    rank = rank4[0:CH]
    val = jnp.where(valid[0:CH], g[0:CH] + 1.0, 0.0)
    for l in range(1, NL):
        s = slice(l * CH, (l + 1) * CH)
        rank = rank + rank4[s]
        val = val + jnp.where(valid[s], g[s] + 1.0, 0.0)
    hi = jnp.floor(val * (1.0 / 64.0))
    lo = val - 64.0 * hi
    pi = (iota((PR, 128), 0) + 1).astype(f32)
    for a in range(CH):
        s = slice(a * 128, (a + 1) * 128)
        rt[:, s] = (rank[a : a + 1] == pi).astype(bf16)
        ev[0:16, s] = (hot[a] * hi[a : a + 1]).astype(bf16)
        ev[16:32, s] = (hot[a] * lo[a : a + 1]).astype(bf16)
    hl = dot(rt[...], ev[...], NT)
    inv = 64.0 * hl[:, :16] + hl[:, 16:] - 1.0
    cp.wait()
    ji = iota((W, 256), 0)

    def window(i, l, w):
        al = base_s[l * 8, 2 * i] & -16
        return pl.multiple_of(al + w * W, 16)

    def grow(i, l):
        k = l * CH + 2 * i
        return jnp.concatenate([gref[pl.ds(k, 1), :], gref[pl.ds(k + 1, 1), :]], axis=1)

    UN = 4
    steps = seg // 256 // UN
    for s in range(NSEG):
        cps[s].wait()

        def body(j, _):
            for u in range(UN):
                i = j * UN + u
                x = emb_v[pl.ds(pl.multiple_of(i * 256, 256), 256), :]
                st = [window(i, l, 0) for l in range(NL)]
                p = jnp.concatenate(
                    [(grow(i, l) - st[l] == ji).astype(f32).astype(bf16) for l in range(NL)], axis=0
                )
                y = dot(p, x).astype(bf16)
                for l in range(NL):
                    C[l, pl.ds(st[l], W), :] = C[l, pl.ds(st[l], W), :] + y[l * W : (l + 1) * W]
            return 0

        lax.fori_loop(s * steps, (s + 1) * steps, body, 0)

    def rest(i, _):
        for l in range(NL):
            b0 = base_s[l * 8, 2 * i]
            need = base_s[l * 8, 2 * i + 2] - (b0 & -16)

            @pl.when(need > W)
            def _():
                x = emb_v[pl.ds(pl.multiple_of(i * 256, 256), 256), :]

                def win(w, _):
                    st = window(i, l, w)
                    y = dot((grow(i, l) - st == ji).astype(f32).astype(bf16), x).astype(bf16)
                    C[l, pl.ds(st, W), :] = C[l, pl.ds(st, W), :] + y
                    return 0

                lax.fori_loop(1, (need + W - 1) // W, win, 0)

        return 0

    @pl.when(jnp.max(over) > W)
    def _():
        lax.fori_loop(0, CH // 2, rest, 0)

    ki = iota((LCAP, LCAP), 1).astype(f32)
    first = iota((LCAP, 128), 1) == 0
    outs = []
    for l in range(NL):
        col = jnp.concatenate([inv[:, t : t + 1] for t in range(l * GL, (l + 1) * GL)], axis=0)
        y = dot((col == ki).astype(f32).astype(bf16), C[l, 0:LCAP, :])
        mark = y[:, 0:128] + jnp.where((col < 0.0) & first, 64.0, 0.0)
        stage[l, :, 0:128] = mark.astype(bf16)
        stage[l, :, 128:D] = y[:, 128:D].astype(bf16)
        cp = pltpu.make_async_copy(stage.at[l], out_ref.at[pl.ds(l * LCAP, LCAP)], osem.at[l])
        cp.start()
        outs.append(cp)
    for cp in outs:
        cp.wait()


def gather(ids, slots, emb):
    return pl.pallas_call(
        gk,
        in_specs=[
            pl.BlockSpec(memory_space=pltpu.VMEM),
            pl.BlockSpec(memory_space=pltpu.VMEM),
            pl.BlockSpec(memory_space=pl.ANY),
        ],
        out_specs=pl.BlockSpec(memory_space=pltpu.HBM),
        out_shape=jax.ShapeDtypeStruct((16 * PR, D), bf16),
        scratch_shapes=[
            pltpu.VMEM((NL, CPAD, D), bf16),
            pltpu.VMEM((ROWS, D), bf16),
            pltpu.VMEM((32, ROWS), bf16),
            pltpu.VMEM((PR, ROWS), bf16),
            pltpu.VMEM((NL * CH, 128), jnp.int32),
            pltpu.VMEM((CH, 16, 128), f32),
            pltpu.VMEM((NL * 8, 128), jnp.int32),
            pltpu.SMEM((NL * 8, 128), jnp.int32),
            pltpu.VMEM((NL, LCAP, D), bf16),
            pltpu.SemaphoreType.DMA((NSEG,)),
            pltpu.SemaphoreType.DMA,
            pltpu.SemaphoreType.DMA((NL,)),
        ],
        compiler_params=pltpu.CompilerParams(vmem_limit_bytes=60 << 20),
    )(ids.reshape(CH, 128), slots.reshape(1, 128), emb)


CAP = 2048
BQ = 512
LOG2E = 1.4426950408889634
VM = pl.BlockSpec(memory_space=pltpu.VMEM)
SM = pl.BlockSpec(memory_space=pltpu.SMEM)
HB = pl.BlockSpec(memory_space=pltpu.HBM)


def rows_of(block, start=0, count=BQ):
    return pl.ds(pl.multiple_of(block % 4 * BQ + start, 128), count)


def position():
    return lax.axis_index("gr"), lax.axis_index("gc")


def query_rows(rows, x_ref, normed, bias, keep_ref, swap_ref, sc_ref):
    cos = dot(normed[rows, :], normed[...], NT)
    w = jnp.exp2(cos * (8.0 * LOG2E) + bias[0:1, :])
    tot = jnp.sum(w, axis=1, keepdims=True)
    nb = dot(w.astype(bf16), x_ref[...])
    un = x_ref[rows, 0:128][:, 0:1].astype(f32) > 32.0
    div = jnp.where(un, 1.0, tot)
    m = jnp.where(un, 0.0, nb / div).astype(bf16)
    lo, hi = m[:, :384], m[:, 384:]
    even = lax.axis_index("gc") == 0
    keep_ref[...] = jnp.where(even, lo, hi)
    swap_ref[...] = jnp.where(even, hi, lo)
    sc_ref[...] = jnp.broadcast_to(jnp.log(div), (rows.size, 128)).T[0:1, :]


def cost(rows):
    return pl.CostEstimate(
        flops=4 * rows * CAP * D, bytes_accessed=4 * CAP * D, transcendentals=rows * CAP
    )


def params(mib=28):
    return pltpu.CompilerParams(vmem_limit_bytes=mib << 20)


def tiles(rows):
    t = jax.ShapeDtypeStruct((rows, 384), bf16)
    return [t, t, jax.ShapeDtypeStruct((1, rows), f32)]


def first_rows(x):
    def kernel(x_ref, normed, bias, *outs):
        for k in range(CAP // 256):
            s = pl.ds(k * 256, 256)
            v = x_ref[s, :].astype(f32)
            sq = jnp.sum(v * v, axis=1, keepdims=True)
            normed[s, :] = (v * lax.rsqrt(sq + 1e-6)).astype(bf16)
        e0 = (iota((8, D), 1) == 0).astype(bf16)
        bias[...] = jnp.where(dot(e0, x_ref[...], NT) > 32.0, -1e30, -8.0 * LOG2E)
        query_rows(rows_of(position()[0] + 2, 0, 512), x_ref, normed, bias, *outs)

    return pl.pallas_call(
        kernel,
        in_specs=[VM],
        out_specs=[VM] * 5,
        out_shape=[
            jax.ShapeDtypeStruct((CAP, D), bf16),
            jax.ShapeDtypeStruct((8, CAP), f32),
            *tiles(512),
        ],
        compiler_params=params(),
        cost_estimate=cost(512),
    )(x)


def more_rows(x, normed, bias, spans):
    def kernel(x_ref, normed, bias, *outs):
        for i, (d, start, count) in enumerate(spans):
            rows = rows_of(position()[0] + d, start, count)
            query_rows(rows, x_ref, normed, bias, *outs[3 * i : 3 * i + 3])

    n = len(spans)
    return pl.pallas_call(
        kernel,
        in_specs=[VM, VM, VM],
        out_specs=[VM] * (3 * n),
        out_shape=[t for _, _, count in spans for t in tiles(count)],
        compiler_params=params(),
        cost_estimate=cost(sum(count for _, _, count in spans)),
    )(x, normed, bias)


def own_block(x, normed, bias, others):
    def kernel(x_ref, normed, bias, c1, c2, c3, out_ref, s0, scores, tile, c0, sem):
        z, c = position()
        query_rows(rows_of(z), x_ref, normed, bias, tile, s0, c0)
        cp = pltpu.make_async_copy(tile, out_ref.at[z * 2 + c], sem)
        cp.start()
        for d, sc in enumerate((c0[...], c1[...], c2[...], c3[...])):
            for h in range(2):
                scores[(z + d) % 4 * 2 + h] = sc
        cp.wait()

    return pl.pallas_call(
        kernel,
        in_specs=[VM] * 6,
        out_specs=[HB, VM, VM],
        out_shape=[
            jax.ShapeDtypeStruct((8, BQ, 384), bf16),
            jax.ShapeDtypeStruct((BQ, 384), bf16),
            jax.ShapeDtypeStruct((8, 1, BQ), f32),
        ],
        scratch_shapes=[
            pltpu.VMEM((BQ, 384), bf16),
            pltpu.VMEM((1, BQ), f32),
            pltpu.SemaphoreType.DMA,
        ],
        compiler_params=params(),
        cost_estimate=cost(BQ),
    )(x, normed, bias, *others)


def place(out, got, scores=None):
    n = len(got)
    k = 0 if scores is None else 1

    def kernel(*refs):
        z, c = position()
        out_ref, sem = refs[n + 1 + k], refs[-1]
        cps = []
        for i, (dz, dc, start, piece) in enumerate(got):
            at = (z + 4 - dz) % 4 * 2 + (c + dc) % 2
            target = out_ref.at[at, pl.ds(start, piece.shape[0])]
            cps.append(pltpu.make_async_copy(refs[i], target, sem.at[i]))
            cps[-1].start()
        if k:
            for q in range(8):
                refs[n + 2 + k][q : q + 1, :] = refs[n + 1][q]
        for cp in cps:
            cp.wait()

    results = [jax.ShapeDtypeStruct(out.shape, out.dtype), jax.ShapeDtypeStruct((8, BQ), f32)]
    return pl.pallas_call(
        kernel,
        in_specs=[VM] * n + [HB] + [VM] * k,
        out_specs=[HB, VM][: 1 + k],
        out_shape=results[: 1 + k],
        input_output_aliases={n: 0},
        scratch_shapes=[pltpu.SemaphoreType.DMA((n,))],
        compiler_params=params(8),
    )(*[p for _, _, _, p in got], out, *([scores] if k else []))


def step(embeddings, cluster_ids, cluster_slots):
    outgoing = gather(cluster_ids, cluster_slots, embeddings)
    arrived = lax.all_to_all(
        outgoing.reshape(16, PR, D), "ingest", split_axis=0, concat_axis=0, tiled=True
    )
    x = arrived.reshape(CAP, D)

    def send(a, dz, dc, start=0):
        pairs = [(i, (i // 2 + dz) % 4 * 2 + (i % 2 + dc) % 2) for i in range(8)]
        return (dz, dc, start, lax.ppermute(a, ("gr", "gc"), pairs))

    normed, bias, k2, s2, c2 = first_rows(x)
    got = [send(k2, 2, 0), send(s2, 2, 1)]
    k1, s1, c1, k3, s3, c3 = more_rows(x, normed, bias, [(1, 0, BQ), (3, 0, BQ)])
    last = [send(s1, 1, 1), send(s3, 3, 1), send(k1, 1, 0), send(k3, 3, 0)]
    out, s0, scores = own_block(x, normed, bias, (c1, c2, c3))
    got += [send(s0, 0, 1)]
    scores = lax.all_to_all(scores, ("gr", "gc"), split_axis=0, concat_axis=0, tiled=True)
    (out,) = place(out, got)
    return tuple(place(out, last, scores))


def solution(mesh):
    return jax.shard_map(
        step,
        mesh=mesh,
        in_specs=(P("ingest", None), P("ingest", None), P()),
        out_specs=(P("ingest", "gr", "gc"), P("ingest", "gr")),
        check_vma=False,
    )
```

```python
import jax
import jax.numpy as jnp
from jax import lax
from jax.experimental import pallas as pl
from jax.experimental.pallas import tpu as pltpu
from jax.sharding import PartitionSpec as P

D = 768
NT = (((1,), (1,)), ((), ()))
NN = (((1,), (0,)), ((), ()))
bf16 = jnp.bfloat16
f32 = jnp.float32


def dot(a, b, dn=NN):
    return lax.dot_general(a, b, dn, preferred_element_type=f32)


def iota(shape, d):
    return lax.broadcasted_iota(jnp.int32, shape, d)


ROWS = 8192
CH = ROWS // 128
NSEG = 4
NL = 4
GL = 16 // NL
W = 48
PR = 128
LCAP = GL * PR
CPAD = LCAP + 64


def gk(ids_ref, slots_ref, emb_ref, out_ref, C, emb_v, ev, rt, gref, rk, base_v, base_s, stage, sem, dsem, osem):
    seg = ROWS // NSEG
    cps = [
        pltpu.make_async_copy(
            emb_ref.at[pl.ds(s * seg, seg)], emb_v.at[pl.ds(s * seg, seg)], sem.at[s]
        )
        for s in range(NSEG)
    ]
    for c in cps:
        c.start()
    C[...] = jnp.zeros_like(C)
    want = iota((16, 128), 0) * 8 + lax.axis_index("gr") * 2 + lax.axis_index("gc")
    cl = jnp.sum(jnp.where(slots_ref[...] == want, iota((16, 128), 1), 0), axis=1, keepdims=True)
    hot = (ids_ref[...][:, None, :] == cl[None, :, :]).astype(f32)
    hotb = hot.astype(bf16).reshape(CH * 16, 128)
    upper = (iota((128, 128), 0) < iota((128, 128), 1)).astype(bf16)
    ones = jnp.ones((128, 128), bf16)
    pre = dot(hotb, upper).reshape(CH, 16, 128)
    tot = dot(hotb, ones).reshape(CH, 16, 128)
    carry = jnp.ones((16, 128), f32)
    for a in range(CH):
        rk[a] = carry + pre[a]
        carry = carry + tot[a]
    own = (hot * rk[...]).astype(bf16).reshape(CH * 16, 128)
    r4 = iota((NL * CH, CH * 16), 0)
    c4 = iota((NL * CH, CH * 16), 1)
    pick = (((c4 >> 4) == (r4 & 63)) & (((c4 & 15) >> 2) == (r4 >> 6))).astype(bf16)
    rank4 = dot(pick, own)
    valid = rank4 > 0.0
    vb = valid.astype(f32).astype(bf16)
    rr = iota((NL * CH, NL * CH), 0)
    cc = iota((NL * CH, NL * CH), 1)
    lower = (((rr >> 6) == (cc >> 6)) & (cc < rr)).astype(bf16)
    tb = dot(vb, ones).astype(bf16)
    g = dot(lower, tb) + dot(vb, upper)
    gref[...] = jnp.where(valid, g, -1e6).astype(jnp.int32)
    trow = dot(jnp.ones((8, 128), bf16), vb, NT).astype(bf16)
    before = (iota((CH, 128), 0) < iota((CH, 128), 1)).astype(bf16)
    after = (iota((CH, 128), 0) < iota((CH, 128), 1) + 2).astype(bf16)
    lane = iota((8, 128), 1)
    chunk = (lane < CH) & ((lane & 1) == 0)
    over = jnp.zeros((8, 128), jnp.int32)
    for l in range(NL):
        counts = trow[:, l * CH : (l + 1) * CH]
        base = dot(counts, before).astype(jnp.int32)
        need = dot(counts, after).astype(jnp.int32) - (base & -16)
        over = jnp.maximum(over, jnp.where(chunk, need, 0))
        base_v[l * 8 : l * 8 + 8] = base
    cp = pltpu.make_async_copy(base_v, base_s, dsem)
    cp.start()
    rank = rank4[0:CH]
    val = jnp.where(valid[0:CH], g[0:CH] + 1.0, 0.0)
    for l in range(1, NL):
        s = slice(l * CH, (l + 1) * CH)
        rank = rank + rank4[s]
        val = val + jnp.where(valid[s], g[s] + 1.0, 0.0)
    hi = jnp.floor(val * (1.0 / 64.0))
    lo = val - 64.0 * hi
    pi = (iota((PR, 128), 0) + 1).astype(f32)
    for a in range(CH):
        s = slice(a * 128, (a + 1) * 128)
        rt[:, s] = (rank[a : a + 1] == pi).astype(bf16)
        ev[0:16, s] = (hot[a] * hi[a : a + 1]).astype(bf16)
        ev[16:32, s] = (hot[a] * lo[a : a + 1]).astype(bf16)
    hl = dot(rt[...], ev[...], NT)
    inv = 64.0 * hl[:, :16] + hl[:, 16:] - 1.0
    cp.wait()
    ji = iota((W, 256), 0)

    def window(i, l, w):
        al = base_s[l * 8, 2 * i] & -16
        return pl.multiple_of(al + w * W, 16)

    def grow(i, l):
        k = l * CH + 2 * i
        return jnp.concatenate([gref[pl.ds(k, 1), :], gref[pl.ds(k + 1, 1), :]], axis=1)

    UN = 8
    for s in range(NSEG):
        cps[s].wait()

        def body(j):
            for u in range(UN):
                i = j * UN + u
                x = emb_v[pl.ds(pl.multiple_of(i * 256, 256), 256), :]
                st = [window(i, l, 0) for l in range(NL)]
                p = jnp.concatenate(
                    [(grow(i, l) - st[l] == ji).astype(f32).astype(bf16) for l in range(NL)], axis=0
                )
                y = dot(p, x).astype(bf16)
                for l in range(NL):
                    C[l, pl.ds(st[l], W), :] = C[l, pl.ds(st[l], W), :] + y[l * W : (l + 1) * W]
            return 0

        body(s)

    def rest(i, _):
        for l in range(NL):
            b0 = base_s[l * 8, 2 * i]
            need = base_s[l * 8, 2 * i + 2] - (b0 & -16)

            @pl.when(need > W)
            def _():
                x = emb_v[pl.ds(pl.multiple_of(i * 256, 256), 256), :]

                def win(w, _):
                    st = window(i, l, w)
                    y = dot((grow(i, l) - st == ji).astype(f32).astype(bf16), x).astype(bf16)
                    C[l, pl.ds(st, W), :] = C[l, pl.ds(st, W), :] + y
                    return 0

                lax.fori_loop(1, (need + W - 1) // W, win, 0)

        return 0

    @pl.when(jnp.max(over) > W)
    def _():
        lax.fori_loop(0, CH // 2, rest, 0)

    ki = iota((LCAP, LCAP), 1).astype(f32)
    first = iota((LCAP, 128), 1) == 0
    outs = []
    for l in range(NL):
        col = jnp.concatenate([inv[:, t : t + 1] for t in range(l * GL, (l + 1) * GL)], axis=0)
        y = dot((col == ki).astype(f32).astype(bf16), C[l, 0:LCAP, :])
        mark = y[:, 0:128] + jnp.where((col < 0.0) & first, 64.0, 0.0)
        stage[l, :, 0:128] = mark.astype(bf16)
        stage[l, :, 128:D] = y[:, 128:D].astype(bf16)
        cp = pltpu.make_async_copy(stage.at[l], out_ref.at[pl.ds(l * LCAP, LCAP)], osem.at[l])
        cp.start()
        outs.append(cp)
    for cp in outs:
        cp.wait()


def gather(ids, slots, emb):
    return pl.pallas_call(
        gk,
        in_specs=[
            pl.BlockSpec(memory_space=pltpu.VMEM),
            pl.BlockSpec(memory_space=pltpu.VMEM),
            pl.BlockSpec(memory_space=pl.ANY),
        ],
        out_specs=pl.BlockSpec(memory_space=pltpu.HBM),
        out_shape=jax.ShapeDtypeStruct((16 * PR, D), bf16),
        scratch_shapes=[
            pltpu.VMEM((NL, CPAD, D), bf16),
            pltpu.VMEM((ROWS, D), bf16),
            pltpu.VMEM((32, ROWS), bf16),
            pltpu.VMEM((PR, ROWS), bf16),
            pltpu.VMEM((NL * CH, 128), jnp.int32),
            pltpu.VMEM((CH, 16, 128), f32),
            pltpu.VMEM((NL * 8, 128), jnp.int32),
            pltpu.SMEM((NL * 8, 128), jnp.int32),
            pltpu.VMEM((NL, LCAP, D), bf16),
            pltpu.SemaphoreType.DMA((NSEG,)),
            pltpu.SemaphoreType.DMA,
            pltpu.SemaphoreType.DMA((NL,)),
        ],
        compiler_params=pltpu.CompilerParams(vmem_limit_bytes=60 << 20),
    )(ids.reshape(CH, 128), slots.reshape(1, 128), emb)


CAP = 2048
BQ = 512
LOG2E = 1.4426950408889634
VM = pl.BlockSpec(memory_space=pltpu.VMEM)
SM = pl.BlockSpec(memory_space=pltpu.SMEM)
HB = pl.BlockSpec(memory_space=pltpu.HBM)


def rows_of(block, start=0, count=BQ):
    return pl.ds(pl.multiple_of(block % 4 * BQ + start, 128), count)


def position():
    return lax.axis_index("gr"), lax.axis_index("gc")


def query_rows(rows, x_ref, normed, bias, keep_ref, swap_ref, sc_ref):
    cos = dot(normed[rows, :], normed[...], NT)
    w = jnp.exp2(cos * (8.0 * LOG2E) + bias[0:1, :])
    tot = jnp.sum(w, axis=1, keepdims=True)
    nb = dot(w.astype(bf16), x_ref[...])
    un = x_ref[rows, 0:128][:, 0:1].astype(f32) > 32.0
    div = jnp.where(un, 1.0, tot)
    m = jnp.where(un, 0.0, nb / div).astype(bf16)
    lo, hi = m[:, :384], m[:, 384:]
    even = lax.axis_index("gc") == 0
    keep_ref[...] = jnp.where(even, lo, hi)
    swap_ref[...] = jnp.where(even, hi, lo)
    sc_ref[...] = jnp.broadcast_to(jnp.log(div), (rows.size, 128)).T[0:1, :]


def cost(rows):
    return pl.CostEstimate(
        flops=4 * rows * CAP * D, bytes_accessed=4 * CAP * D, transcendentals=rows * CAP
    )


def params(mib=28):
    return pltpu.CompilerParams(vmem_limit_bytes=mib << 20)


def tiles(rows):
    t = jax.ShapeDtypeStruct((rows, 384), bf16)
    return [t, t, jax.ShapeDtypeStruct((1, rows), f32)]


def first_rows(x):
    def kernel(x_ref, normed, bias, *outs):
        for k in range(CAP // 256):
            s = pl.ds(k * 256, 256)
            v = x_ref[s, :].astype(f32)
            sq = jnp.sum(v * v, axis=1, keepdims=True)
            normed[s, :] = (v * lax.rsqrt(sq + 1e-6)).astype(bf16)
        e0 = (iota((8, D), 1) == 0).astype(bf16)
        bias[...] = jnp.where(dot(e0, x_ref[...], NT) > 32.0, -1e30, -8.0 * LOG2E)
        query_rows(rows_of(position()[0] + 2, 0, 512), x_ref, normed, bias, *outs)

    return pl.pallas_call(
        kernel,
        in_specs=[VM],
        out_specs=[VM] * 5,
        out_shape=[
            jax.ShapeDtypeStruct((CAP, D), bf16),
            jax.ShapeDtypeStruct((8, CAP), f32),
            *tiles(512),
        ],
        compiler_params=params(),
        cost_estimate=cost(512),
    )(x)


def more_rows(x, normed, bias, spans):
    def kernel(x_ref, normed, bias, *outs):
        for i, (d, start, count) in enumerate(spans):
            rows = rows_of(position()[0] + d, start, count)
            query_rows(rows, x_ref, normed, bias, *outs[3 * i : 3 * i + 3])

    n = len(spans)
    return pl.pallas_call(
        kernel,
        in_specs=[VM, VM, VM],
        out_specs=[VM] * (3 * n),
        out_shape=[t for _, _, count in spans for t in tiles(count)],
        compiler_params=params(),
        cost_estimate=cost(sum(count for _, _, count in spans)),
    )(x, normed, bias)


def own_block(x, normed, bias, others):
    def kernel(x_ref, normed, bias, c1, c2, c3, out_ref, s0, scores, tile, c0, sem):
        z, c = position()
        query_rows(rows_of(z), x_ref, normed, bias, tile, s0, c0)
        cp = pltpu.make_async_copy(tile, out_ref.at[z * 2 + c], sem)
        cp.start()
        for d, sc in enumerate((c0[...], c1[...], c2[...], c3[...])):
            for h in range(2):
                scores[(z + d) % 4 * 2 + h] = sc
        cp.wait()

    return pl.pallas_call(
        kernel,
        in_specs=[VM] * 6,
        out_specs=[HB, VM, VM],
        out_shape=[
            jax.ShapeDtypeStruct((8, BQ, 384), bf16),
            jax.ShapeDtypeStruct((BQ, 384), bf16),
            jax.ShapeDtypeStruct((8, 1, BQ), f32),
        ],
        scratch_shapes=[
            pltpu.VMEM((BQ, 384), bf16),
            pltpu.VMEM((1, BQ), f32),
            pltpu.SemaphoreType.DMA,
        ],
        compiler_params=params(),
        cost_estimate=cost(BQ),
    )(x, normed, bias, *others)


def place(out, got, scores=None):
    n = len(got)
    k = 0 if scores is None else 1

    def kernel(*refs):
        z, c = position()
        out_ref, sem = refs[n + 1 + k], refs[-1]
        cps = []
        for i, (dz, dc, start, piece) in enumerate(got):
            at = (z + 4 - dz) % 4 * 2 + (c + dc) % 2
            target = out_ref.at[at, pl.ds(start, piece.shape[0])]
            cps.append(pltpu.make_async_copy(refs[i], target, sem.at[i]))
            cps[-1].start()
        if k:
            for q in range(8):
                refs[n + 2 + k][q : q + 1, :] = refs[n + 1][q]
        for cp in cps:
            cp.wait()

    results = [jax.ShapeDtypeStruct(out.shape, out.dtype), jax.ShapeDtypeStruct((8, BQ), f32)]
    return pl.pallas_call(
        kernel,
        in_specs=[VM] * n + [HB] + [VM] * k,
        out_specs=[HB, VM][: 1 + k],
        out_shape=results[: 1 + k],
        input_output_aliases={n: 0},
        scratch_shapes=[pltpu.SemaphoreType.DMA((n,))],
        compiler_params=params(8),
    )(*[p for _, _, _, p in got], out, *([scores] if k else []))


def step(embeddings, cluster_ids, cluster_slots):
    outgoing = gather(cluster_ids, cluster_slots, embeddings)
    arrived = lax.all_to_all(
        outgoing.reshape(16, PR, D), "ingest", split_axis=0, concat_axis=0, tiled=True
    )
    x = arrived.reshape(CAP, D)

    def send(a, dz, dc, start=0):
        pairs = [(i, (i // 2 + dz) % 4 * 2 + (i % 2 + dc) % 2) for i in range(8)]
        return (dz, dc, start, lax.ppermute(a, ("gr", "gc"), pairs))

    normed, bias, k2, s2, c2 = first_rows(x)
    got = [send(k2, 2, 0), send(s2, 2, 1)]
    k1, s1, c1, k3, s3, c3 = more_rows(x, normed, bias, [(1, 0, BQ), (3, 0, BQ)])
    near = [send(s1, 1, 1), send(s3, 3, 1)]
    last = [send(k1, 1, 0), send(k3, 3, 0)]
    out, s0, scores = own_block(x, normed, bias, (c1, c2, c3))
    got += [send(s0, 0, 1)]
    scores = lax.all_to_all(scores, ("gr", "gc"), split_axis=0, concat_axis=0, tiled=True)
    (out,) = place(out, got)
    (out,) = place(out, near)
    return tuple(place(out, last, scores))


def solution(mesh):
    return jax.shard_map(
        step,
        mesh=mesh,
        in_specs=(P("ingest", None), P("ingest", None), P()),
        out_specs=(P("ingest", "gr", "gc"), P("ingest", "gr")),
        check_vma=False,
    )
```

```python
import jax
import jax.numpy as jnp
from jax import lax
from jax.experimental import pallas as pl
from jax.experimental.pallas import tpu as pltpu
from jax.sharding import PartitionSpec as P

D = 768
NT = (((1,), (1,)), ((), ()))
NN = (((1,), (0,)), ((), ()))
bf16 = jnp.bfloat16
f32 = jnp.float32


def dot(a, b, dn=NN):
    return lax.dot_general(a, b, dn, preferred_element_type=f32)


def iota(shape, d):
    return lax.broadcasted_iota(jnp.int32, shape, d)


ROWS = 8192
CH = ROWS // 128
NSEG = 4
NL = 4
GL = 16 // NL
W = 48
PR = 128
LCAP = GL * PR
CPAD = LCAP + 64


def gk(ids_ref, slots_ref, emb_ref, out_ref, C, emb_v, ev, rt, gref, rk, base_v, base_s, stage, sem, dsem, osem):
    seg = ROWS // NSEG
    cps = [
        pltpu.make_async_copy(
            emb_ref.at[pl.ds(s * seg, seg)], emb_v.at[pl.ds(s * seg, seg)], sem.at[s]
        )
        for s in range(NSEG)
    ]
    for c in cps:
        c.start()
    C[...] = jnp.zeros_like(C)
    want = iota((16, 128), 0) * 8 + lax.axis_index("gr") * 2 + lax.axis_index("gc")
    cl = jnp.sum(jnp.where(slots_ref[...] == want, iota((16, 128), 1), 0), axis=1, keepdims=True)
    hot = (ids_ref[...][:, None, :] == cl[None, :, :]).astype(f32)
    hotb = hot.astype(bf16).reshape(CH * 16, 128)
    upper = (iota((128, 128), 0) < iota((128, 128), 1)).astype(bf16)
    ones = jnp.ones((128, 128), bf16)
    both = jnp.concatenate([upper, ones], axis=1)
    sums = dot(hotb, both)
    pre = sums[:, :128].reshape(CH, 16, 128)
    tot = sums[:, 128:].reshape(CH, 16, 128)
    carry = jnp.ones((16, 128), f32)
    for a in range(CH):
        rk[a] = carry + pre[a]
        carry = carry + tot[a]
    own = (hot * rk[...]).astype(bf16).reshape(CH * 16, 128)
    r4 = iota((NL * CH, CH * 16), 0)
    c4 = iota((NL * CH, CH * 16), 1)
    pick = (((c4 >> 4) == (r4 & 63)) & (((c4 & 15) >> 2) == (r4 >> 6))).astype(bf16)
    rank4 = dot(pick, own)
    valid = rank4 > 0.0
    vb = valid.astype(f32).astype(bf16)
    rr = iota((NL * CH, NL * CH), 0)
    cc = iota((NL * CH, NL * CH), 1)
    lower = (((rr >> 6) == (cc >> 6)) & (cc < rr)).astype(bf16)
    vsums = dot(vb, both)
    g = dot(lower, vsums[:, 128:].astype(bf16)) + vsums[:, :128]
    gref[...] = jnp.where(valid, g, -1e6).astype(jnp.int32)
    trow = dot(jnp.ones((8, 128), bf16), vb, NT).astype(bf16)
    before = (iota((CH, 128), 0) < iota((CH, 128), 1)).astype(bf16)
    after = (iota((CH, 128), 0) < iota((CH, 128), 1) + 2).astype(bf16)
    lane = iota((8, 128), 1)
    chunk = (lane < CH) & ((lane & 1) == 0)
    over = jnp.zeros((8, 128), jnp.int32)
    for l in range(NL):
        counts = trow[:, l * CH : (l + 1) * CH]
        base = dot(counts, before).astype(jnp.int32)
        need = dot(counts, after).astype(jnp.int32) - (base & -16)
        over = jnp.maximum(over, jnp.where(chunk, need, 0))
        base_v[l * 8 : l * 8 + 8] = base
    cp = pltpu.make_async_copy(base_v, base_s, dsem)
    cp.start()
    rank = rank4[0:CH]
    val = jnp.where(valid[0:CH], g[0:CH] + 1.0, 0.0)
    for l in range(1, NL):
        s = slice(l * CH, (l + 1) * CH)
        rank = rank + rank4[s]
        val = val + jnp.where(valid[s], g[s] + 1.0, 0.0)
    hi = jnp.floor(val * (1.0 / 64.0))
    lo = val - 64.0 * hi
    pi = (iota((PR, 128), 0) + 1).astype(f32)
    for a in range(CH):
        s = slice(a * 128, (a + 1) * 128)
        rt[:, s] = (rank[a : a + 1] == pi).astype(bf16)
        ev[0:16, s] = (hot[a] * hi[a : a + 1]).astype(bf16)
        ev[16:32, s] = (hot[a] * lo[a : a + 1]).astype(bf16)
    hl = dot(rt[...], ev[...], NT)
    inv = 64.0 * hl[:, :16] + hl[:, 16:] - 1.0
    cp.wait()
    ji = iota((W, 256), 0)

    def window(i, l, w):
        al = base_s[l * 8, 2 * i] & -16
        return pl.multiple_of(al + w * W, 16)

    def grow(i, l):
        k = l * CH + 2 * i
        return jnp.concatenate([gref[pl.ds(k, 1), :], gref[pl.ds(k + 1, 1), :]], axis=1)

    UN = 8
    for s in range(NSEG):
        cps[s].wait()

        def body(j):
            for u in range(UN):
                i = j * UN + u
                x = emb_v[pl.ds(pl.multiple_of(i * 256, 256), 256), :]
                st = [window(i, l, 0) for l in range(NL)]
                p = jnp.concatenate(
                    [(grow(i, l) - st[l] == ji).astype(f32).astype(bf16) for l in range(NL)], axis=0
                )
                y = dot(p, x).astype(bf16)
                for l in range(NL):
                    C[l, pl.ds(st[l], W), :] = C[l, pl.ds(st[l], W), :] + y[l * W : (l + 1) * W]
            return 0

        body(s)

    def rest(i, _):
        for l in range(NL):
            b0 = base_s[l * 8, 2 * i]
            need = base_s[l * 8, 2 * i + 2] - (b0 & -16)

            @pl.when(need > W)
            def _():
                x = emb_v[pl.ds(pl.multiple_of(i * 256, 256), 256), :]

                def win(w, _):
                    st = window(i, l, w)
                    y = dot((grow(i, l) - st == ji).astype(f32).astype(bf16), x).astype(bf16)
                    C[l, pl.ds(st, W), :] = C[l, pl.ds(st, W), :] + y
                    return 0

                lax.fori_loop(1, (need + W - 1) // W, win, 0)

        return 0

    @pl.when(jnp.max(over) > W)
    def _():
        lax.fori_loop(0, CH // 2, rest, 0)

    ki = iota((LCAP, LCAP), 1).astype(f32)
    first = iota((LCAP, 128), 1) == 0
    outs = []
    for l in range(NL):
        col = jnp.concatenate([inv[:, t : t + 1] for t in range(l * GL, (l + 1) * GL)], axis=0)
        y = dot((col == ki).astype(f32).astype(bf16), C[l, 0:LCAP, :])
        mark = y[:, 0:128] + jnp.where((col < 0.0) & first, 64.0, 0.0)
        stage[l, :, 0:128] = mark.astype(bf16)
        stage[l, :, 128:D] = y[:, 128:D].astype(bf16)
        cp = pltpu.make_async_copy(stage.at[l], out_ref.at[pl.ds(l * LCAP, LCAP)], osem.at[l])
        cp.start()
        outs.append(cp)
    for cp in outs:
        cp.wait()


def gather(ids, slots, emb):
    return pl.pallas_call(
        gk,
        in_specs=[
            pl.BlockSpec(memory_space=pltpu.VMEM),
            pl.BlockSpec(memory_space=pltpu.VMEM),
            pl.BlockSpec(memory_space=pl.ANY),
        ],
        out_specs=pl.BlockSpec(memory_space=pltpu.HBM),
        out_shape=jax.ShapeDtypeStruct((16 * PR, D), bf16),
        scratch_shapes=[
            pltpu.VMEM((NL, CPAD, D), bf16),
            pltpu.VMEM((ROWS, D), bf16),
            pltpu.VMEM((32, ROWS), bf16),
            pltpu.VMEM((PR, ROWS), bf16),
            pltpu.VMEM((NL * CH, 128), jnp.int32),
            pltpu.VMEM((CH, 16, 128), f32),
            pltpu.VMEM((NL * 8, 128), jnp.int32),
            pltpu.SMEM((NL * 8, 128), jnp.int32),
            pltpu.VMEM((NL, LCAP, D), bf16),
            pltpu.SemaphoreType.DMA((NSEG,)),
            pltpu.SemaphoreType.DMA,
            pltpu.SemaphoreType.DMA((NL,)),
        ],
        compiler_params=pltpu.CompilerParams(vmem_limit_bytes=60 << 20),
    )(ids.reshape(CH, 128), slots.reshape(1, 128), emb)


CAP = 2048
BQ = 512
LOG2E = 1.4426950408889634
VM = pl.BlockSpec(memory_space=pltpu.VMEM)
SM = pl.BlockSpec(memory_space=pltpu.SMEM)
HB = pl.BlockSpec(memory_space=pltpu.HBM)


def rows_of(block, start=0, count=BQ):
    return pl.ds(pl.multiple_of(block % 4 * BQ + start, 128), count)


def position():
    return lax.axis_index("gr"), lax.axis_index("gc")


def query_rows(rows, x_ref, normed, bias, keep_ref, swap_ref, sc_ref):
    cos = dot(normed[rows, :], normed[...], NT)
    w = jnp.exp2(cos * (8.0 * LOG2E) + bias[0:1, :])
    tot = jnp.sum(w, axis=1, keepdims=True)
    nb = dot(w.astype(bf16), x_ref[...])
    un = x_ref[rows, 0:128][:, 0:1].astype(f32) > 32.0
    div = jnp.where(un, 1.0, tot)
    m = jnp.where(un, 0.0, nb / div).astype(bf16)
    lo, hi = m[:, :384], m[:, 384:]
    even = lax.axis_index("gc") == 0
    keep_ref[...] = jnp.where(even, lo, hi)
    swap_ref[...] = jnp.where(even, hi, lo)
    sc_ref[...] = jnp.broadcast_to(jnp.log(div), (rows.size, 128)).T[0:1, :]


def cost(rows):
    return pl.CostEstimate(
        flops=4 * rows * CAP * D, bytes_accessed=4 * CAP * D, transcendentals=rows * CAP
    )


def params(mib=28):
    return pltpu.CompilerParams(vmem_limit_bytes=mib << 20)


def tiles(rows):
    t = jax.ShapeDtypeStruct((rows, 384), bf16)
    return [t, t, jax.ShapeDtypeStruct((1, rows), f32)]


def first_rows(x):
    def kernel(x_ref, normed, bias, *outs):
        for k in range(CAP // 256):
            s = pl.ds(k * 256, 256)
            v = x_ref[s, :].astype(f32)
            sq = jnp.sum(v * v, axis=1, keepdims=True)
            normed[s, :] = (v * lax.rsqrt(sq + 1e-6)).astype(bf16)
        e0 = (iota((8, 128), 1) == 0).astype(bf16)
        bias[...] = jnp.where(dot(e0, x_ref[:, 0:128], NT) > 32.0, -1e30, -8.0 * LOG2E)
        query_rows(rows_of(position()[0] + 2, 0, 512), x_ref, normed, bias, *outs)

    return pl.pallas_call(
        kernel,
        in_specs=[VM],
        out_specs=[VM] * 5,
        out_shape=[
            jax.ShapeDtypeStruct((CAP, D), bf16),
            jax.ShapeDtypeStruct((8, CAP), f32),
            *tiles(512),
        ],
        compiler_params=params(),
        cost_estimate=cost(512),
    )(x)


def more_rows(x, normed, bias, spans):
    def kernel(x_ref, normed, bias, *outs):
        for i, (d, start, count) in enumerate(spans):
            rows = rows_of(position()[0] + d, start, count)
            query_rows(rows, x_ref, normed, bias, *outs[3 * i : 3 * i + 3])

    n = len(spans)
    return pl.pallas_call(
        kernel,
        in_specs=[VM, VM, VM],
        out_specs=[VM] * (3 * n),
        out_shape=[t for _, _, count in spans for t in tiles(count)],
        compiler_params=params(),
        cost_estimate=cost(sum(count for _, _, count in spans)),
    )(x, normed, bias)


def own_block(x, normed, bias, others):
    def kernel(x_ref, normed, bias, c1, c2, c3, out_ref, s0, scores, tile, c0, sem):
        z, c = position()
        query_rows(rows_of(z), x_ref, normed, bias, tile, s0, c0)
        cp = pltpu.make_async_copy(tile, out_ref.at[z * 2 + c], sem)
        cp.start()
        for d, sc in enumerate((c0[...], c1[...], c2[...], c3[...])):
            for h in range(2):
                scores[(z + d) % 4 * 2 + h] = sc
        cp.wait()

    return pl.pallas_call(
        kernel,
        in_specs=[VM] * 6,
        out_specs=[HB, VM, VM],
        out_shape=[
            jax.ShapeDtypeStruct((8, BQ, 384), bf16),
            jax.ShapeDtypeStruct((BQ, 384), bf16),
            jax.ShapeDtypeStruct((8, 1, BQ), f32),
        ],
        scratch_shapes=[
            pltpu.VMEM((BQ, 384), bf16),
            pltpu.VMEM((1, BQ), f32),
            pltpu.SemaphoreType.DMA,
        ],
        compiler_params=params(),
        cost_estimate=cost(BQ),
    )(x, normed, bias, *others)


def place(out, got, scores=None):
    n = len(got)
    k = 0 if scores is None else 1

    def kernel(*refs):
        z, c = position()
        out_ref, sem = refs[n + 1 + k], refs[-1]
        cps = []
        for i, (dz, dc, start, piece) in enumerate(got):
            at = (z + 4 - dz) % 4 * 2 + (c + dc) % 2
            target = out_ref.at[at, pl.ds(start, piece.shape[0])]
            cps.append(pltpu.make_async_copy(refs[i], target, sem.at[i]))
            cps[-1].start()
        if k:
            for q in range(8):
                refs[n + 2 + k][q : q + 1, :] = refs[n + 1][q]
        for cp in cps:
            cp.wait()

    results = [jax.ShapeDtypeStruct(out.shape, out.dtype), jax.ShapeDtypeStruct((8, BQ), f32)]
    return pl.pallas_call(
        kernel,
        in_specs=[VM] * n + [HB] + [VM] * k,
        out_specs=[HB, VM][: 1 + k],
        out_shape=results[: 1 + k],
        input_output_aliases={n: 0},
        scratch_shapes=[pltpu.SemaphoreType.DMA((n,))],
        compiler_params=params(8),
    )(*[p for _, _, _, p in got], out, *([scores] if k else []))


def step(embeddings, cluster_ids, cluster_slots):
    outgoing = gather(cluster_ids, cluster_slots, embeddings)
    arrived = lax.all_to_all(
        outgoing.reshape(16, PR, D), "ingest", split_axis=0, concat_axis=0, tiled=True
    )
    x = arrived.reshape(CAP, D)

    def send(a, dz, dc, start=0):
        pairs = [(i, (i // 2 + dz) % 4 * 2 + (i % 2 + dc) % 2) for i in range(8)]
        return (dz, dc, start, lax.ppermute(a, ("gr", "gc"), pairs))

    normed, bias, k2, s2, c2 = first_rows(x)
    got = [send(k2, 2, 0), send(s2, 2, 1)]
    k1, s1, c1, k3, s3, c3 = more_rows(x, normed, bias, [(1, 0, BQ), (3, 0, BQ)])
    near = [send(s1, 1, 1), send(s3, 3, 1)]
    last = [send(k1, 1, 0), send(k3, 3, 0)]
    out, s0, scores = own_block(x, normed, bias, (c1, c2, c3))
    got += [send(s0, 0, 1)]
    scores = lax.all_to_all(scores, ("gr", "gc"), split_axis=0, concat_axis=0, tiled=True)
    (out,) = place(out, got)
    (out,) = place(out, near)
    return tuple(place(out, last, scores))


def solution(mesh):
    return jax.shard_map(
        step,
        mesh=mesh,
        in_specs=(P("ingest", None), P("ingest", None), P()),
        out_specs=(P("ingest", "gr", "gc"), P("ingest", "gr")),
        check_vma=False,
    )
```
